512 devices in a mesh: ctx: 64 (over z, y), head: 8 (over x, core).
Axes of the slice: x: 4, y: 8, z: 8, core: 2. Of those that a mesh axis runs over, the one named last changes fastest.
Arguments:
- queries: bfloat16 [49152, 3072], P(('ctx', 'head')), may hold values from -20 to 20
- keys: bfloat16 [49152, 3072], P(('ctx', 'head')), may hold values from -6 to 6
- values: bfloat16 [49152, 3072], P(('ctx', 'head')), may hold values from -6 to 6
- page_blocks: int32 [64, 2], replicated, may hold values from 1 to 5, as said below
- page_links: int32 [128, 16], replicated, may hold values from 0 to 127, as said below
- global_blocks: int32 [2], replicated, may hold values from 0 to 383
Outputs:
- attended: bfloat16 [49152, 3072], P(('ctx', 'head'))
The draws below stay inside these ranges and needn't reach their ends.
Inputs may be any that keep to these rules, and one draw needn't show every extreme that they name: `page_links`: all 32 links of the pages of one ctx index name pages of distinct other ctx indices. `page_blocks`: each row sums to 6; some ctx index has a page of exactly 5 blocks.
All inputs are finite; a program needn't handle non-finite values.
Results may differ from the reference program's by a relative error of at most 0.0048.
Values may be sent and summed in bfloat16 or wider, within the bound.
A program may use at most 128 MiB of HBM per device.

```python
import jax
import jax.numpy as jnp
from jax import lax

HEADS = 24
HD = 128
BLK = 128
TOK_CTX = 768
PAGES_DEV = 2
GROWS = 64
GB = 2
LINKS = 16
TOKENS = 49152
PAGES = 128
N_CTX = 64


def shared_keys(key):
    base = jax.random.fold_in(key, 11)
    return jax.random.truncated_normal(base, -6.0, 6.0, (TOKENS, HEADS * HD), jnp.float32)


def draw_keys(key, part):
    return shared_keys(key).astype(jnp.bfloat16)


def draw_queries(key, part):
    base = jax.random.fold_in(key, 23)
    drawn = jax.random.truncated_normal(base, -6.0, 6.0, (TOKENS, HEADS * HD), jnp.float32)
    return drawn.astype(jnp.bfloat16)


def draw_page_blocks(key, part):
    total_blocks = TOK_CTX // BLK
    first = jax.random.randint(jax.random.fold_in(key, 41), (N_CTX,), 1, total_blocks)
    first = jnp.where(jnp.arange(N_CTX) == 0, total_blocks - 1, first)
    return jnp.stack((first, total_blocks - first), axis=1).astype(jnp.int32)


def draw_page_links(key, part):

    def reader_links(reader):
        reader_key = jax.random.fold_in(jax.random.fold_in(key, 37), reader)
        others = jax.random.permutation(reader_key, N_CTX - 1)[:PAGES_DEV * LINKS]
        sources = others + (others >= reader).astype(jnp.int32)
        which = jax.random.randint(jax.random.fold_in(reader_key, 1), (PAGES_DEV * LINKS,), 0, PAGES_DEV)
        return (sources * PAGES_DEV + which).reshape(PAGES_DEV, LINKS)
    return jax.vmap(reader_links)(jnp.arange(N_CTX, dtype=jnp.int32)).reshape(PAGES, LINKS).astype(jnp.int32)


def level_of(rng, shape, pieces, low, top_value):
    level, own = 1.0, jax.random.fold_in(rng, 6)
    for dim, shards_of in pieces:
        steps = jnp.exp(jax.random.uniform(jax.random.fold_in(own, dim), (shards_of,), jnp.float32, low / len(pieces), top_value / len(pieces)))
        level = level * jnp.repeat(steps, shape[dim] // shards_of).reshape([-1 if axis == dim else 1 for axis in range(len(shape))])
    return level


def gaussian(rng, dims, scale, limit, pieces=(), kind=jnp.bfloat16):
    drawn = scale * jax.random.normal(rng, dims, jnp.float32)
    if pieces:
        drawn = drawn * level_of(rng, dims, pieces, -0.22, 0.18)
    return jnp.clip(drawn, -limit, limit).astype(kind)


def setup_inputs(seed: int = 0) -> dict:
    streams_of = jax.random.split(jax.random.key(seed), 7)
    return {
        "queries": draw_queries(jax.random.fold_in(streams_of[6], 71), 0),
        "keys": draw_keys(jax.random.fold_in(streams_of[6], 71), 0),
        "values": gaussian(streams_of[2], (TOKENS, HEADS * HD), 1.0, 6.0, ((0, 512),)),
        "page_blocks": draw_page_blocks(jax.random.fold_in(streams_of[6], 71), 0),
        "page_links": draw_page_links(jax.random.fold_in(streams_of[6], 71), 0),
        "global_blocks": jax.random.randint(streams_of[5], (GB,), 0, TOKENS // BLK).astype(jnp.int32),
    }


def reference(queries, keys, values, page_blocks, page_links, global_blocks):
    blocks_ctx = TOK_CTX // BLK
    width = HEADS * HD
    ctx_count = page_blocks.shape[0]
    base_blocks = (jnp.arange(ctx_count, dtype=jnp.int32) * blocks_ctx)[:, None]
    local_starts = (jnp.cumsum(page_blocks, axis=1) - page_blocks).astype(jnp.int32)
    page_start = (local_starts + base_blocks).reshape(-1).astype(jnp.int32)
    local_ids = jnp.arange(blocks_ctx, dtype=jnp.int32)
    local_page = jnp.sum((local_ids[None, :, None] >= local_starts[:, None, :]).astype(jnp.int32), axis=2) - 1
    block_page = (local_page + (jnp.arange(ctx_count, dtype=jnp.int32) * PAGES_DEV)[:, None]).reshape(-1).astype(jnp.int32)
    span = GROWS // GB
    glob_k = jnp.concatenate([lax.dynamic_slice_in_dim(keys, (global_blocks[i] * BLK).astype(jnp.int32), span, 0) for i in range(GB)], 0)
    glob_v = jnp.concatenate([lax.dynamic_slice_in_dim(values, (global_blocks[i] * BLK).astype(jnp.int32), span, 0) for i in range(GB)], 0)
    scale = HD ** -0.5

    def one_block(block):
        ctx_id = (block // blocks_ctx).astype(jnp.int32)
        page = block_page[block]
        q_rows = lax.dynamic_slice_in_dim(queries, (block * BLK).astype(jnp.int32), BLK, 0)
        own_k = lax.dynamic_slice_in_dim(keys, (ctx_id * TOK_CTX).astype(jnp.int32), TOK_CTX, 0)
        own_v = lax.dynamic_slice_in_dim(values, (ctx_id * TOK_CTX).astype(jnp.int32), TOK_CTX, 0)
        own_pages = jnp.repeat(lax.dynamic_slice_in_dim(block_page, (ctx_id * blocks_ctx).astype(jnp.int32), blocks_ctx, 0), BLK)
        link_starts = (page_start[page_links[page]] * BLK).astype(jnp.int32)
        link_k = jax.vmap(lambda s: lax.dynamic_slice_in_dim(keys, s, BLK, 0))(link_starts).reshape(LINKS * BLK, width)
        link_v = jax.vmap(lambda s: lax.dynamic_slice_in_dim(values, s, BLK, 0))(link_starts).reshape(LINKS * BLK, width)
        all_k = jnp.concatenate((own_k, glob_k, link_k), 0)
        all_v = jnp.concatenate((own_v, glob_v, link_v), 0)
        visible = jnp.concatenate((own_pages == page, jnp.ones((GROWS + LINKS * BLK,), bool)), 0)
        q_heads = q_rows.reshape(BLK, HEADS, HD).astype(jnp.float32)
        k_heads = all_k.reshape(-1, HEADS, HD).astype(jnp.float32)
        v_heads = all_v.reshape(-1, HEADS, HD).astype(jnp.float32)
        scores = jnp.einsum("qhd,khd->hqk", q_heads, k_heads) * scale
        scores = jnp.where(visible[None, None, :], scores, -1e30)
        row_max = jnp.max(scores, axis=2, keepdims=True)
        weights = jnp.exp(scores - row_max)
        total = jnp.sum(weights, axis=2)
        rounded = lax.optimization_barrier(weights.astype(jnp.bfloat16)).astype(jnp.float32)
        mixed = jnp.einsum("hqk,khd->qhd", rounded, v_heads)
        mixed = mixed / jnp.transpose(total)[:, :, None]
        return mixed.reshape(BLK, width).astype(jnp.bfloat16)

    result = lax.map(one_block, jnp.arange(TOKENS // BLK, dtype=jnp.int32))
    return result.reshape(TOKENS, width)
```

```python
import functools

import jax
import jax.numpy as jnp
from jax import lax
from jax.experimental import pallas as pl
from jax.experimental.pallas import tpu as pltpu
from jax.sharding import PartitionSpec as P

HD = 128
BLK = 128
PAGES_DEV = 2
GROWS = 64
GB = 2
RING_Y = 8
MESH = pl.DeviceIdType.MESH
MASKED = -1e30
LOG2E = 1.4426950408889634


def ring_offsets(n):
    out = []
    for d in range(1, (n + 1) // 2):
        out += [d, -d]
    if n % 2 == 0:
        out.append(n // 2)
    return out


def body(
    nz,
    ny,
    nh,
    starts_ref,
    codes_ref,
    gblk_ref,
    q_ref,
    k_ref,
    v_ref,
    out_ref,
    qx,
    kx,
    vx,
    ga,
    gb,
    picked,
    g1,
    g2,
    ks,
    vs,
    bias,
    tops,
    totals,
    mixed,
    ob,
    send_sem,
    recv_sem,
):
    rows, width = qx.shape
    rl = rows // nh
    half = BLK // 2
    span = GROWS // GB
    n_heads = width // HD
    n_blocks = rows // BLK
    me = lax.axis_index("ctx")
    mh = lax.axis_index("head")
    z, y = me // ny, me % ny
    rate = HD**-0.5 * LOG2E

    def wrap(v, n):
        return lax.rem(v + 2 * n, n)

    def ctx_at(dz, dy):
        return wrap(z + dz, nz) * ny + wrap(y + dy, ny)

    neighbours = [ctx_at(1, 0), ctx_at(-1, 0), ctx_at(0, 1), ctx_at(0, -1)]
    peers = [lax.rem(mh + r, nh) for r in range(1, nh)]
    barrier = pltpu.get_barrier_semaphore()
    for n in neighbours:
        pl.semaphore_signal(barrier, inc=1, device_id={"ctx": n}, device_id_type=MESH)
    for p in peers:
        pl.semaphore_signal(barrier, inc=1, device_id={"head": p}, device_id_type=MESH)
    pl.semaphore_wait(barrier, len(neighbours) + len(peers))

    sems = {}
    sends = []

    def sem_id(key):
        return sems.setdefault(key, len(sems))

    def remote(key, src, dst, device):
        k = sem_id(key)
        return pltpu.make_async_remote_copy(
            src_ref=src,
            dst_ref=dst,
            send_sem=send_sem.at[k],
            recv_sem=recv_sem.at[k],
            device_id=device,
            device_id_type=MESH,
        )

    def row_slot(h):
        return pl.ds(pl.multiple_of(h * rl, 16), rl)

    def col_slot(h):
        return pl.ds(pl.multiple_of(h * width, HD), width)

    def spread(name, src, dst):
        local = pltpu.make_async_copy(
            src.at[:, col_slot(mh)], dst.at[row_slot(mh), :], recv_sem.at[sem_id((name, 0))]
        )
        local.start()
        for r, p in enumerate(peers, 1):
            c = remote((name, r), src.at[:, col_slot(p)], dst.at[row_slot(mh), :], {"head": p})
            c.start()
            sends.append(c)

        def wait():
            local.wait()
            for r in range(1, nh):
                slot = dst.at[row_slot(lax.rem(mh + nh - r, nh)), :]
                remote((name, r), slot, slot, {"head": peers[r - 1]}).wait_recv()

        return wait

    wait_k = spread("k", k_ref, kx)
    wait_v = spread("v", v_ref, vx)
    wait_q = spread("q", q_ref, qx)
    wait_k()
    wait_v()

    start1 = starts_ref[me, 0]

    def choose(index, options):
        out = options[0][1]()
        for value, load in options[1:]:
            out = jnp.where(index == value, load(), out)
        return out

    for kv, src in enumerate((kx, vx)):
        for part, g in enumerate((ga, gb)):
            lo = part * half
            g[me, 0, kv] = src[lo : lo + half, :]
            g[me, 1, kv] = choose(
                start1,
                [
                    (j, lambda j=j: src[j * BLK + lo : j * BLK + lo + half, :])
                    for j in range(1, n_blocks)
                ],
            )
    owner = [gblk_ref[i] // n_blocks for i in range(GB)]
    place = [gblk_ref[i] % n_blocks for i in range(GB)]

    def load_global_candidates():
        for i in range(GB):
            for kv, src in enumerate((kx, vx)):
                g1[z, i, kv] = choose(
                    place[i],
                    [(j, lambda j=j: src[j * BLK : j * BLK + span, :]) for j in range(n_blocks)],
                )

    waited = set()
    n_picked = [0]

    class Stream:
        def __init__(s, name, ref, axis, off, kind, far=0):
            s.name, s.ref, s.axis, s.off, s.kind, s.far = name, ref, axis, off, kind, far
            s.steps = (nz if axis == "z" else ny) // 2

        def place(s, rel):
            return (rel, s.off) if s.axis == "z" else (s.off, rel)

        def slot(s, rel):
            if s.kind == "rows":
                return s.ref.at[wrap(z + rel, nz) if s.axis == "z" else wrap(y + rel, ny)]
            return s.ref.at[ctx_at(*s.place(rel))]

        def to(s, d):
            return {"ctx": ctx_at(d, 0) if s.axis == "z" else ctx_at(0, d)}

        def hops(s, d):
            return s.steps if not s.far or d == s.far else s.steps - 1

        def picks(s, d, t):
            return bool(s.far) and t == s.hops(d) - 1

        def piece(s, rel, d, t):
            ref = s.slot(rel)
            if s.far:
                return ref.at[pl.ds(0, 1)] if s.picks(d, t) else ref
            if t == s.steps - 1:
                return ref.at[pl.ds(0 if d > 0 else 1, 1)]
            return ref

        def send(s, d, t):
            if t >= s.hops(d):
                return
            if t > 0:
                s.wait(d, t - 1)
            dst = s.piece(-d * t, d, t)
            src = dst
            if s.picks(d, t):
                k = n_picked[0]
                n_picked[0] += 1
                full = s.slot(-d * t)
                code = codes_ref[s.to(d)["ctx"], ctx_at(*s.place(-d * t))]
                for kv in range(2):
                    picked[k, 0, kv] = jnp.where(code % 2 == 0, full[1, kv], full[0, kv])
                src = picked.at[k]
            c = remote((s.name, d, t), src, dst, s.to(d))
            c.start()
            sends.append(c)

        def wait(s, d, t):
            if t >= s.hops(d) or (s.name, d, t) in waited:
                return
            waited.add((s.name, d, t))
            ref = s.piece(-d * (t + 1), d, t)
            remote((s.name, d, t), ref, ref, s.to(d)).wait_recv()

        def need(s, rel):
            if abs(rel) == s.steps:
                s.wait(1, s.steps - 1)
                s.wait(-1, s.steps - 1)
            elif rel < 0:
                s.wait(1, -rel - 1)
            elif rel > 0:
                s.wait(-1, rel - 1)

        def arrivals(s, t):
            out = []
            if t >= s.steps:
                return out
            if s.far or t < s.steps - 1:
                for d in (1, -1):
                    if t < s.hops(d):
                        out.append((s, -d * (t + 1), s.picks(d, t)))
                        s.wait(d, t)
            else:
                s.wait(1, t)
                s.wait(-1, t)
                out.append((s, s.steps, False))
            return out

        def finish(s):
            for d in (1, -1):
                for t in range(s.hops(d)):
                    s.wait(d, t)

    def attend(n, first=False):
        def block(b, carry):
            at = pl.ds(pl.multiple_of(b * BLK, BLK), BLK)
            mask = jnp.where(b >= start1, bias[1:2, :n], bias[0:1, :n])
            for h in range(n_heads):
                cols = slice(h * HD, (h + 1) * HD)
                k = kx[:, cols] if first else ks[:n, cols]
                v = vx[:, cols] if first else vs[:n, cols]
                s = lax.dot_general(
                    qx[at, cols], k, (((1,), (1,)), ((), ())), preferred_element_type=jnp.float32
                )
                s = s * rate + mask
                top = jnp.max(s, axis=1, keepdims=True)
                if not first:
                    before = tops[h, at, :]
                    after = jnp.maximum(before, top)
                    top = after[:, :1]
                else:
                    after = jnp.broadcast_to(top, (BLK, HD))
                w = jnp.exp2(s - top)
                total = jnp.sum(w, axis=1, keepdims=True)
                mix = jnp.dot(w.astype(jnp.bfloat16), v, preferred_element_type=jnp.float32)
                if first:
                    totals[h, at, :] = jnp.broadcast_to(total, (BLK, HD))
                    mixed[h, at, :] = mix
                else:
                    decay = jnp.exp2(before - after)
                    totals[h, at, :] = totals[h, at, :] * decay + total
                    mixed[h, at, :] = mixed[h, at, :] * decay + mix
                tops[h, at, :] = after
            return carry

        lax.fori_loop(0, n_blocks, block, 0)

    lane = lax.broadcasted_iota(jnp.int32, (1, 2 * half), 1)

    def absorb(arrived):
        if not arrived:
            return
        level = []
        for j, (s, rel, single) in enumerate(arrived):
            ref = s.slot(rel)
            code = codes_ref[me, ctx_at(*s.place(rel))]
            at = slice(j * half, (j + 1) * half)
            for kv, dst in ((0, ks), (1, vs)):
                dst[at, :] = (
                    ref[0, kv] if single else jnp.where(code % 2 == 0, ref[1, kv], ref[0, kv])
                )
            level.append(
                [
                    jnp.where((code + 1) // 2 == page + 1, 0.0, MASKED)
                    for page in range(PAGES_DEV)
                ]
            )
        n = len(arrived) * half
        if len(arrived) % 2:
            at = slice(n, n + half)
            ks[at, :] = jnp.zeros((half, width), ks.dtype)
            vs[at, :] = jnp.zeros((half, width), vs.dtype)
            level.append([MASKED] * PAGES_DEV)
            n += half
        for page in range(PAGES_DEV):
            for j in range(0, len(level), 2):
                bias[page : page + 1, j * half : (j + 2) * half] = jnp.where(
                    lane < half, level[j][page], level[j + 1][page]
                )
        attend(n)

    def attend_own():
        token = lax.broadcasted_iota(jnp.int32, (1, rows), 1)
        for page in range(PAGES_DEV):
            bias[page : page + 1, :rows] = jnp.where(
                (token >= start1 * BLK) == (page == 1), 0.0, MASKED
            )
        attend(rows, first=True)

    def attend_global():
        for i in range(GB):
            at = slice(i * span, (i + 1) * span)
            for kv, dst in ((0, ks), (1, vs)):
                dst[at, :] = choose(
                    owner[i] % ny, [(j, lambda j=j: g2[j, i, kv]) for j in range(ny)]
                )
        for page in range(PAGES_DEV):
            bias[page : page + 1, :GROWS] = jnp.zeros((1, GROWS), jnp.float32)
        attend(GROWS)

    a1 = Stream("a1", ga, "z", 0, "pages")
    b1 = Stream("b1", gb, "y", 0, "pages")
    za, yb = ring_offsets(nz), ring_offsets(ny)
    a2 = {o: Stream(("a2", o), ga, "y", o, "pages", 1 - 2 * (i % 2)) for i, o in enumerate([0] + za)}
    b2 = {o: Stream(("b2", o), gb, "z", o, "pages", 1 - 2 * (i % 2)) for i, o in enumerate([0] + yb)}
    r1 = Stream("r1", g1, "z", 0, "rows")
    r2 = Stream("r2", g2, "y", 0, "rows")

    def pairs(offs):
        out = []
        while len(offs) > 3:
            out.append(offs[:2])
            offs = offs[2:]
        return out + ([offs] if offs else [])

    za, yb = pairs(za), pairs(yb)
    groups = [[a1, b1, a2[0], b2[0]]]
    for i in range(max(len(za), len(yb))):
        g = [a2[o] for o in (za[i] if i < len(za) else [])]
        groups.append(g + [b2[o] for o in (yb[i] if i < len(yb) else [])])
    groups[min(1, len(groups) - 2)].append(r1)
    groups[-1].append(r2)
    pending = []
    for gi, g in enumerate(groups):
        for t in range(max(s.steps for s in g)):
            if r1 in g and t == 0:
                load_global_candidates()
            if gi == len(groups) - 1 and t == 0:
                r1.finish()
                for i in range(GB):
                    for kv in range(2):
                        g2[y, i, kv] = choose(
                            owner[i] // ny, [(j, lambda j=j: g1[j, i, kv]) for j in range(nz)]
                        )
            for s in g:
                if t == 0 and s.off != 0:
                    (a1 if s.axis == "y" else b1).need(s.off)
                for d in (1, -1):
                    s.send(d, t)
            if gi == 0 and t == 0:
                wait_q()
                attend_own()
            arrived = []
            for s, ts in pending:
                arrived += s.arrivals(ts)
            absorb(arrived)
            pending = [(s, t) for s in g if s.kind == "pages"]
    r2.finish()
    attend_global()
    arrived = []
    for s, ts in pending:
        arrived += s.arrivals(ts)
    absorb(arrived)
    for s in [a1, b1, r1] + list(a2.values()) + list(b2.values()):
        s.finish()

    for h in range(n_heads):
        cols = slice(h * HD, (h + 1) * HD)
        ob[:, cols] = (mixed[h] / totals[h]).astype(jnp.bfloat16)

    local = pltpu.make_async_copy(
        ob.at[row_slot(mh), :], out_ref.at[:, col_slot(mh)], recv_sem.at[sem_id(("o", 0))]
    )
    local.start()
    for r, p in enumerate(peers, 1):
        c = remote(("o", r), ob.at[row_slot(p), :], out_ref.at[:, col_slot(mh)], {"head": p})
        c.start()
        sends.append(c)
    local.wait()
    for r in range(1, nh):
        slot = out_ref.at[:, col_slot(lax.rem(mh + nh - r, nh))]
        remote(("o", r), slot, slot, {"head": peers[r - 1]}).wait_recv()
    for c in sends:
        c.wait_send()


def shards(nz, ny, nh, queries, keys, values, page_blocks, page_links, global_blocks):
    rl, full = queries.shape
    rows, width = rl * nh, full // nh
    n_ctx = nz * ny
    n_heads = width // HD
    half = BLK // 2
    span = GROWS // GB
    bf, f32 = jnp.bfloat16, jnp.float32
    reader = jnp.arange(PAGES_DEV, dtype=jnp.int32)[None, :, None]
    links = page_links.reshape(n_ctx, PAGES_DEV, -1)
    value = 1 + links % PAGES_DEV + PAGES_DEV * reader
    source = jnp.arange(n_ctx, dtype=jnp.int32)
    codes = jnp.sum(
        jnp.where((links // PAGES_DEV)[..., None] == source, value[..., None], 0), axis=(1, 2)
    )
    n_sems = 4 * nh + (nz + ny) + nz * ny * 2 + (nz + ny)
    most = max(rows, 12 * half)
    smem = pl.BlockSpec(memory_space=pltpu.SMEM)
    hbm = pl.BlockSpec(memory_space=pl.ANY)
    return pl.pallas_call(
        functools.partial(body, nz, ny, nh),
        out_shape=jax.ShapeDtypeStruct((rl, full), bf),
        in_specs=[smem, smem, smem, hbm, hbm, hbm],
        out_specs=hbm,
        scratch_shapes=[
            pltpu.VMEM((rows, width), bf),
            pltpu.VMEM((rows, width), bf),
            pltpu.VMEM((rows, width), bf),
            pltpu.VMEM((n_ctx, PAGES_DEV, 2, half, width), bf),
            pltpu.VMEM((n_ctx, PAGES_DEV, 2, half, width), bf),
            pltpu.VMEM((2 * (nz + ny), 1, 2, half, width), bf),
            pltpu.VMEM((nz, GB, 2, span, width), bf),
            pltpu.VMEM((ny, GB, 2, span, width), bf),
            pltpu.VMEM((most, width), bf),
            pltpu.VMEM((most, width), bf),
            pltpu.VMEM((PAGES_DEV, most), f32),
            pltpu.VMEM((n_heads, rows, HD), f32),
            pltpu.VMEM((n_heads, rows, HD), f32),
            pltpu.VMEM((n_heads, rows, HD), f32),
            pltpu.VMEM((rows, width), bf),
            pltpu.SemaphoreType.DMA((n_sems,)),
            pltpu.SemaphoreType.DMA((n_sems,)),
        ],
        compiler_params=pltpu.CompilerParams(
            collective_id=0, has_side_effects=True, vmem_limit_bytes=60 * 1024 * 1024
        ),
        name="page_attention",
    )(page_blocks, codes, global_blocks, queries, keys, values)


def solution(mesh):
    nh = mesh.shape["head"]
    ny = RING_Y
    nz = mesh.shape["ctx"] // ny
    return jax.shard_map(
        functools.partial(shards, nz, ny, nh),
        mesh=mesh,
        in_specs=(
            P(("ctx", "head"), None),
            P(("ctx", "head"), None),
            P(("ctx", "head"), None),
            P(),
            P(),
            P(),
        ),
        out_specs=P(("ctx", "head"), None),
        check_vma=False,
    )
```

```python
import functools

import jax
import jax.numpy as jnp
from jax import lax
from jax.experimental import pallas as pl
from jax.experimental.pallas import tpu as pltpu
from jax.sharding import PartitionSpec as P

HD = 128
BLK = 128
PAGES_DEV = 2
GROWS = 64
GB = 2
RING_Y = 8
MESH = pl.DeviceIdType.MESH
MASKED = -1e30
LOG2E = 1.4426950408889634


def ring_offsets(n):
    out = []
    for d in range(1, (n + 1) // 2):
        out += [d, -d]
    if n % 2 == 0:
        out.append(n // 2)
    return out


def body(
    nz,
    ny,
    nh,
    codes_ref,
    gblk_ref,
    q_ref,
    k_ref,
    v_ref,
    out_ref,
    qx,
    kx,
    vx,
    ga,
    gb,
    picked,
    own_piece,
    got_z,
    got_y,
    picked_rows,
    ks,
    vt,
    marks,
    qmarks,
    tops,
    totals,
    mixed,
    ob,
    send_sem,
    recv_sem,
):
    rows, width = qx.shape
    rl = rows // nh
    half = BLK // 2
    span = GROWS // GB
    n_heads = width // HD
    n_blocks = rows // BLK
    me = lax.axis_index("ctx")
    mh = lax.axis_index("head")
    z, y = me // ny, me % ny
    rate = HD**-0.5 * LOG2E

    def wrap(v, n):
        return lax.rem(v + 2 * n, n)

    def ctx_at(dz, dy):
        return wrap(z + dz, nz) * ny + wrap(y + dy, ny)

    neighbours = [ctx_at(0, 1), ctx_at(0, -1)] + [ctx_at(r, 0) for r in range(1, nz)]
    peers = [lax.rem(mh + r, nh) for r in range(1, nh)]
    barrier = pltpu.get_barrier_semaphore()
    for n in neighbours:
        pl.semaphore_signal(barrier, inc=1, device_id={"ctx": n}, device_id_type=MESH)
    for p in peers:
        pl.semaphore_signal(barrier, inc=1, device_id={"head": p}, device_id_type=MESH)
    pl.semaphore_wait(barrier, len(neighbours) + len(peers))

    sems = {}
    sends = []

    def sem_id(key):
        return sems.setdefault(key, len(sems))

    def remote(key, src, dst, device):
        k = sem_id(key)
        return pltpu.make_async_remote_copy(
            src_ref=src,
            dst_ref=dst,
            send_sem=send_sem.at[k],
            recv_sem=recv_sem.at[k],
            device_id=device,
            device_id_type=MESH,
        )

    def row_slot(h):
        return pl.ds(pl.multiple_of(h * rl, 16), rl)

    def col_slot(h):
        return pl.ds(pl.multiple_of(h * width, HD), width)

    def spread(name, src, dst):
        local = pltpu.make_async_copy(
            src.at[:, col_slot(mh)], dst.at[row_slot(mh), :], recv_sem.at[sem_id((name, 0))]
        )
        local.start()
        for r, p in enumerate(peers, 1):
            c = remote((name, r), src.at[:, col_slot(p)], dst.at[row_slot(mh), :], {"head": p})
            c.start()
            sends.append(c)

        def wait():
            local.wait()
            for r in range(1, nh):
                slot = dst.at[row_slot(lax.rem(mh + nh - r, nh)), :]
                remote((name, r), slot, slot, {"head": peers[r - 1]}).wait_recv()

        return wait

    wait_k = spread("k", k_ref, kx)
    wait_v = spread("v", v_ref, vx)
    wait_q = spread("q", q_ref, qx)
    wait_k()
    wait_v()

    start1 = codes_ref[me, me]

    def choose(index, options):
        out = options[0][1]()
        for value, load in options[1:]:
            out = jnp.where(index == value, load(), out)
        return out

    for kv, src in enumerate((kx, vx)):
        for part, g in enumerate((ga, gb)):
            lo = part * half
            g[me, 0, kv] = src[lo : lo + half, :]
            g[me, 1, kv] = choose(
                start1,
                [
                    (j, lambda j=j: src[j * BLK + lo : j * BLK + lo + half, :])
                    for j in range(1, n_blocks)
                ],
            )
    owner = [gblk_ref[i] // n_blocks for i in range(GB)]
    place = [gblk_ref[i] % n_blocks for i in range(GB)]

    piece_rows = own_piece.shape[1]
    per = span // piece_rows
    pieces = [(i, kv, r) for i in range(GB) for kv in range(2) for r in range(per)]

    def send_candidates():
        for n, (i, kv, r) in enumerate(pieces):
            src = (kx, vx)[kv]
            lo = r * piece_rows
            own_piece[n] = choose(
                place[i],
                [
                    (j, lambda j=j: src[j * BLK + lo : j * BLK + lo + piece_rows, :])
                    for j in range(n_blocks)
                ],
            )
        got_z[z] = own_piece[z]
        for r in range(1, nz):
            zz = wrap(z + r, nz)
            c = remote(("g", r), own_piece.at[zz], got_z.at[z], {"ctx": zz * ny + y})
            c.start()
            sends.append(c)

    def pick_z():
        for r in range(1, nz):
            ref = got_z.at[wrap(z - r, nz)]
            remote(("g", r), ref, ref, {"ctx": ctx_at(-r, 0)}).wait_recv()
        o = owner[0]
        for i in range(1, GB):
            o = jnp.where(z >= i * (nz // GB), owner[i], o)
        got_y[y] = choose(o // ny, [(j, lambda j=j: got_z[j]) for j in range(nz)])

    def pick_y():
        r1.finish()
        o = owner[0]
        for i in range(1, GB):
            o = jnp.where(z >= i * (nz // GB), owner[i], o)
        picked_rows[z] = choose(o % ny, [(j, lambda j=j: got_y[j]) for j in range(ny)])

    def global_entries():
        r2.finish()

        def load(lo):
            out = []
            for kv in range(2):
                own = [n for n, q in enumerate(pieces) if q[1] == kv]
                out.append(jnp.concatenate([picked_rows[n] for n in own], axis=0)[lo : lo + half])
            return out

        return [
            (functools.partial(load, lo), [0.0] * PAGES_DEV) for lo in range(0, GROWS, half)
        ]

    waited = set()
    n_picked = [0]

    class Stream:
        def __init__(s, name, ref, axis, off, kind, far=0):
            s.name, s.ref, s.axis, s.off, s.kind, s.far = name, ref, axis, off, kind, far
            s.steps = (nz if axis == "z" else ny) // 2
            s.single = kind == "pages" and far != 0

        def place(s, rel):
            return (rel, s.off) if s.axis == "z" else (s.off, rel)

        def slot(s, rel):
            if s.kind == "rows":
                return s.ref.at[wrap(z + rel, nz) if s.axis == "z" else wrap(y + rel, ny)]
            return s.ref.at[ctx_at(*s.place(rel))]

        def to(s, d):
            return {"ctx": ctx_at(d, 0) if s.axis == "z" else ctx_at(0, d)}

        def hops(s, d):
            return s.steps if not s.far or d == s.far else s.steps - 1

        def picks(s, d, t):
            return s.single and t == s.hops(d) - 1

        def piece(s, rel, d, t):
            ref = s.slot(rel)
            if s.far:
                return ref.at[pl.ds(0, 1)] if s.picks(d, t) else ref
            if t == s.steps - 1:
                return ref.at[pl.ds(0 if d > 0 else 1, 1)]
            return ref

        def send(s, d, t):
            if t >= s.hops(d):
                return
            if t > 0:
                s.wait(d, t - 1)
            dst = s.piece(-d * t, d, t)
            src = dst
            if s.picks(d, t):
                k = n_picked[0]
                n_picked[0] += 1
                full = s.slot(-d * t)
                code = codes_ref[s.to(d)["ctx"], ctx_at(*s.place(-d * t))]
                for kv in range(2):
                    picked[k, 0, kv] = jnp.where(code % 2 == 0, full[1, kv], full[0, kv])
                src = picked.at[k]
            c = remote((s.name, d, t), src, dst, s.to(d))
            c.start()
            sends.append(c)

        def wait(s, d, t):
            if t >= s.hops(d) or (s.name, d, t) in waited:
                return
            waited.add((s.name, d, t))
            ref = s.piece(-d * (t + 1), d, t)
            remote((s.name, d, t), ref, ref, s.to(d)).wait_recv()

        def need(s, rel):
            if abs(rel) == s.steps:
                s.wait(1, s.steps - 1)
                s.wait(-1, s.steps - 1)
            elif rel < 0:
                s.wait(1, -rel - 1)
            elif rel > 0:
                s.wait(-1, rel - 1)

        def arrivals(s, t):
            out = []
            if t >= s.steps:
                return out
            if s.far or t < s.steps - 1:
                for d in (1, -1):
                    if t < s.hops(d):
                        out.append(page_entry(s, -d * (t + 1), s.picks(d, t)))
                        s.wait(d, t)
            else:
                s.wait(1, t)
                s.wait(-1, t)
                out.append(page_entry(s, s.steps, False))
            return out

        def finish(s):
            for d in (1, -1):
                for t in range(s.hops(d)):
                    s.wait(d, t)

    out_sems = [sem_id(("o", r)) for r in range(nh)]
    local = pltpu.make_async_copy(
        ob.at[row_slot(mh), :], out_ref.at[:, col_slot(mh)], recv_sem.at[out_sems[0]]
    )

    def hand_out(b):
        for h in range(n_heads):
            for lo in range(b * tile, (b + 1) * tile, BLK):
                at = slice(lo, lo + BLK)
                out = mixed[h, :, at] / totals[h, :, at]
                ob[at, h * HD : (h + 1) * HD] = out.T.astype(jnp.bfloat16)
        for p in range(b * tile // rl, (b + 1) * tile // rl):

            @pl.when(mh == p)
            def _():
                local.start()

            @pl.when(mh != p)
            def _():
                at = out_sems[0] + lax.rem(p - mh + nh, nh)
                pltpu.make_async_remote_copy(
                    src_ref=ob.at[row_slot(p), :],
                    dst_ref=out_ref.at[:, col_slot(mh)],
                    send_sem=send_sem.at[at],
                    recv_sem=recv_sem.at[at],
                    device_id={"head": jnp.int32(p)},
                    device_id_type=MESH,
                ).start()

    tile = 2 * BLK if rows % (2 * BLK) == 0 else rows

    def page_marks(n, first_row):
        row = lax.broadcasted_iota(jnp.int32, (n, HD), 0) + first_row
        page = jnp.where(row >= start1 * BLK, 1, 0)
        return page == lax.broadcasted_iota(jnp.int32, (n, HD), 1)

    def attend(n, keys, first=False, last=False):
        def block(b, carry):
            at = pl.ds(pl.multiple_of(b * tile, tile), tile)
            for h in range(n_heads):
                cols = slice(h * HD, (h + 1) * HD)
                s = lax.dot_general(
                    jnp.concatenate((keys[:n, cols], marks[:n, :]), axis=1),
                    jnp.concatenate((qx[at, cols], qmarks[at, :]), axis=1),
                    (((1,), (1,)), ((), ())),
                    preferred_element_type=jnp.float32,
                )
                s = s * rate
                top = jnp.max(s, axis=0, keepdims=True)
                if not first:
                    before = tops[h, :, at]
                    top = jnp.maximum(before, top)
                w = jnp.exp2(s - top)
                total = jnp.sum(w, axis=0, keepdims=True)
                mix = jnp.dot(
                    vt[cols, :n], w.astype(jnp.bfloat16), preferred_element_type=jnp.float32
                )
                if not first:
                    decay = jnp.exp2(before - top)
                    total = totals[h, :, at] * decay + total
                    mix = mixed[h, :, at] * decay + mix
                totals[h, :, at] = total
                mixed[h, :, at] = mix
                tops[h, :, at] = top
            return carry

        if not last:
            lax.fori_loop(0, rows // tile, block, 0)
            return
        for b in range(rows // tile):
            block(b, 0)
            hand_out(b)

    lane = lax.broadcasted_iota(jnp.int32, (half, HD), 1)

    def absorb(entries, last=False):
        if not entries:
            return
        zero = jnp.zeros((half, width), jnp.bfloat16)
        if len(entries) % 2:
            entries = entries + [(lambda: (zero, zero), [MASKED] * PAGES_DEV)]
        for j in range(0, len(entries), 2):
            pair = []
            for i, (load, level) in enumerate(entries[j : j + 2], j):
                k, v = load()
                ks[i * half : (i + 1) * half, :] = k
                marks[i * half : (i + 1) * half, :] = jnp.where(
                    lane == 0, level[0], jnp.where(lane == 1, level[1], 0.0)
                ).astype(jnp.bfloat16)
                pair.append(v)
            vt[:, j * half : (j + 2) * half] = jnp.concatenate(pair, axis=0).T
        attend(len(entries) * half, ks, last=last)

    def page_entry(s, rel, single):
        ref = s.slot(rel)
        code = codes_ref[me, ctx_at(*s.place(rel))]

        def load():
            if single:
                return ref[0, 0], ref[0, 1]
            return [jnp.where(code % 2 == 0, ref[1, kv], ref[0, kv]) for kv in range(2)]

        level = [
            jnp.where((code + 1) // 2 == page + 1, 0.0, MASKED) for page in range(PAGES_DEV)
        ]
        return load, level

    def attend_own():
        qmarks[...] = jnp.where(page_marks(rows, 0), 1.0, 0.0).astype(jnp.bfloat16)
        marks[:rows, :] = jnp.where(
            page_marks(rows, 0) | (lax.broadcasted_iota(jnp.int32, (rows, HD), 1) >= PAGES_DEV),
            0.0,
            MASKED,
        ).astype(jnp.bfloat16)
        for b in range(n_blocks):
            at = slice(b * BLK, (b + 1) * BLK)
            vt[:, at] = vx[at, :].T
        attend(rows, kx, first=True)

    a1 = Stream("a1", ga, "z", 0, "pages")
    b1 = Stream("b1", gb, "y", 0, "pages")
    za, yb = ring_offsets(nz), ring_offsets(ny)
    a2 = {o: Stream(("a2", o), ga, "y", o, "pages", 1 - 2 * (i % 2)) for i, o in enumerate([0] + za)}
    b2 = {o: Stream(("b2", o), gb, "z", o, "pages", 1 - 2 * (i % 2)) for i, o in enumerate([0] + yb)}
    r1 = Stream("r1", got_y, "y", 0, "rows", 1)
    r2 = Stream("r2", picked_rows, "z", 0, "rows", -1)

    def pairs(offs):
        out = []
        while len(offs) > 3:
            out.append(offs[:2])
            offs = offs[2:]
        return out + ([offs] if offs else [])

    za, yb = pairs(za), pairs(yb)
    groups = [[a1, b1, a2[0], b2[0]]]
    for i in range(max(len(za), len(yb))):
        g = [a2[o] for o in (za[i] if i < len(za) else [])]
        groups.append(g + [b2[o] for o in (yb[i] if i < len(yb) else [])])
    rounds = []
    for gi, g in enumerate(groups):
        for t in range(max(s.steps for s in g)):
            if gi > 0 and t == 0 and len(rounds) > 1:
                rounds[-1] += [(s, t) for s in g]
            else:
                rounds.append([(s, t) for s in g])
    last = len(rounds) - 1
    z_round, y_round = min(2, last), min(6, last)
    row_streams = []

    def push_rows(everything=False):
        for entry in row_streams:
            while entry[1] < entry[0].steps:
                for d in (1, -1):
                    entry[0].send(d, entry[1])
                entry[1] += 1
                if not everything:
                    break

    pending = []
    globals_done = False
    for n, todo in enumerate(rounds):
        for s, t in todo:
            if t == 0 and s.off != 0:
                (a1 if s.axis == "y" else b1).need(s.off)
            for d in (1, -1):
                s.send(d, t)
        if n == 0:
            send_candidates()
        if n == z_round:
            pick_z()
            row_streams.append([r1, 0])
        if n == y_round:
            push_rows(True)
            pick_y()
            row_streams.append([r2, 0])
        push_rows()
        if n == min(1, last):
            wait_q()
            attend_own()
        if n > 0:
            arrived = []
            for s, t in pending:
                arrived += s.arrivals(t)
            if n == y_round + 5:
                push_rows(True)
                arrived += global_entries()
                globals_done = True
            absorb(arrived)
        pending = todo
    arrived = []
    for s, t in pending:
        arrived += s.arrivals(t)
    if not globals_done:
        push_rows(True)
        arrived += global_entries()
    absorb(arrived, True)
    for s in [a1, b1, r1] + list(a2.values()) + list(b2.values()):
        s.finish()

    local.wait()
    for r in range(1, nh):
        slot = out_ref.at[:, col_slot(lax.rem(mh + nh - r, nh))]
        remote(("o", r), slot, slot, {"head": peers[r - 1]}).wait_recv()
        mine = ob.at[row_slot(peers[r - 1]), :]
        remote(("o", r), mine, mine, {"head": peers[r - 1]}).wait_send()
    for c in sends:
        c.wait_send()


def shards(nz, ny, nh, queries, keys, values, page_blocks, page_links, global_blocks):
    rl, full = queries.shape
    rows, width = rl * nh, full // nh
    n_ctx = nz * ny
    n_heads = width // HD
    half = BLK // 2
    span = GROWS // GB
    bf, f32 = jnp.bfloat16, jnp.float32
    reader = jnp.arange(PAGES_DEV, dtype=jnp.int32)[None, :, None]
    links = page_links.reshape(n_ctx, PAGES_DEV, -1)
    value = 1 + links % PAGES_DEV + PAGES_DEV * reader
    source = jnp.arange(n_ctx, dtype=jnp.int32)
    codes = jnp.sum(
        jnp.where((links // PAGES_DEV)[..., None] == source, value[..., None], 0), axis=(1, 2)
    )
    codes = jnp.where(source[:, None] == source, page_blocks[:, :1], codes)
    n_sems = 4 * nh + 3 * (nz + ny) + nz * ny * 2
    piece_rows = span * GB * 2 // nz
    most = max(rows, 16 * half)
    smem = pl.BlockSpec(memory_space=pltpu.SMEM)
    hbm = pl.BlockSpec(memory_space=pl.ANY)
    return pl.pallas_call(
        functools.partial(body, nz, ny, nh),
        out_shape=jax.ShapeDtypeStruct((rl, full), bf),
        in_specs=[smem, smem, hbm, hbm, hbm],
        out_specs=hbm,
        scratch_shapes=[
            pltpu.VMEM((rows, width), bf),
            pltpu.VMEM((rows, width), bf),
            pltpu.VMEM((rows, width), bf),
            pltpu.VMEM((n_ctx, PAGES_DEV, 2, half, width), bf),
            pltpu.VMEM((n_ctx, PAGES_DEV, 2, half, width), bf),
            pltpu.VMEM((2 * (nz + ny), 1, 2, half, width), bf),
            pltpu.VMEM((nz, piece_rows, width), bf),
            pltpu.VMEM((nz, piece_rows, width), bf),
            pltpu.VMEM((ny, piece_rows, width), bf),
            pltpu.VMEM((nz, piece_rows, width), bf),
            pltpu.VMEM((most, width), bf),
            pltpu.VMEM((width, most), bf),
            pltpu.VMEM((most, HD), bf),
            pltpu.VMEM((rows, HD), bf),
            pltpu.VMEM((n_heads, 1, rows), f32),
            pltpu.VMEM((n_heads, 1, rows), f32),
            pltpu.VMEM((n_heads, HD, rows), f32),
            pltpu.VMEM((rows, width), bf),
            pltpu.SemaphoreType.DMA((n_sems,)),
            pltpu.SemaphoreType.DMA((n_sems,)),
        ],
        compiler_params=pltpu.CompilerParams(
            collective_id=0, has_side_effects=True, vmem_limit_bytes=60 * 1024 * 1024
        ),
        name="page_attention",
    )(codes, global_blocks, queries, keys, values)


def solution(mesh):
    nh = mesh.shape["head"]
    ny = RING_Y
    nz = mesh.shape["ctx"] // ny
    return jax.shard_map(
        functools.partial(shards, nz, ny, nh),
        mesh=mesh,
        in_specs=(
            P(("ctx", "head"), None),
            P(("ctx", "head"), None),
            P(("ctx", "head"), None),
            P(),
            P(),
            P(),
        ),
        out_specs=P(("ctx", "head"), None),
        check_vma=False,
    )
```

```python
import functools

import jax
import jax.numpy as jnp
from jax import lax
from jax.experimental import pallas as pl
from jax.experimental.pallas import tpu as pltpu
from jax.sharding import PartitionSpec as P

HD = 128
BLK = 128
PAGES_DEV = 2
GROWS = 64
GB = 2
RING_Y = 8
MESH = pl.DeviceIdType.MESH
MASKED = -1e30
LOG2E = 1.4426950408889634


def ring_offsets(n):
    out = []
    for d in range(1, (n + 1) // 2):
        out += [d, -d]
    if n % 2 == 0:
        out.append(n // 2)
    return out


def body(
    nz,
    ny,
    nh,
    codes_ref,
    gblk_ref,
    q_ref,
    k_ref,
    v_ref,
    out_ref,
    qx,
    kx,
    vx,
    ga,
    gb,
    picked,
    own_piece,
    got_z,
    got_y,
    picked_rows,
    ks,
    vt,
    marks,
    qmarks,
    tops,
    totals,
    mixed,
    ob,
    send_sem,
    recv_sem,
):
    rows, width = qx.shape
    rl = rows // nh
    half = BLK // 2
    span = GROWS // GB
    n_heads = width // HD
    n_blocks = rows // BLK
    me = lax.axis_index("ctx")
    mh = lax.axis_index("head")
    z, y = me // ny, me % ny
    rate = HD**-0.5 * LOG2E

    def wrap(v, n):
        return lax.rem(v + 2 * n, n)

    def ctx_at(dz, dy):
        return wrap(z + dz, nz) * ny + wrap(y + dy, ny)

    neighbours = [ctx_at(0, 1), ctx_at(0, -1)] + [ctx_at(r, 0) for r in range(1, nz)]
    peers = [lax.rem(mh + r, nh) for r in range(1, nh)]
    barrier = pltpu.get_barrier_semaphore()
    for n in neighbours:
        pl.semaphore_signal(barrier, inc=1, device_id={"ctx": n}, device_id_type=MESH)
    for p in peers:
        pl.semaphore_signal(barrier, inc=1, device_id={"head": p}, device_id_type=MESH)
    pl.semaphore_wait(barrier, len(neighbours) + len(peers))

    sems = {}
    sends = []

    def sem_id(key):
        return sems.setdefault(key, len(sems))

    def remote(key, src, dst, device):
        k = sem_id(key)
        return pltpu.make_async_remote_copy(
            src_ref=src,
            dst_ref=dst,
            send_sem=send_sem.at[k],
            recv_sem=recv_sem.at[k],
            device_id=device,
            device_id_type=MESH,
        )

    def row_slot(h):
        return pl.ds(pl.multiple_of(h * rl, 16), rl)

    def col_slot(h):
        return pl.ds(pl.multiple_of(h * width, HD), width)

    def spread(name, src, dst):
        local = pltpu.make_async_copy(
            src.at[:, col_slot(mh)], dst.at[row_slot(mh), :], recv_sem.at[sem_id((name, 0))]
        )
        local.start()
        for r, p in enumerate(peers, 1):
            c = remote((name, r), src.at[:, col_slot(p)], dst.at[row_slot(mh), :], {"head": p})
            c.start()
            sends.append(c)

        def wait():
            local.wait()
            for r in range(1, nh):
                slot = dst.at[row_slot(lax.rem(mh + nh - r, nh)), :]
                remote((name, r), slot, slot, {"head": peers[r - 1]}).wait_recv()

        return wait

    wait_k = spread("k", k_ref, kx)
    wait_v = spread("v", v_ref, vx)
    wait_q = spread("q", q_ref, qx)
    wait_k()
    wait_v()

    start1 = codes_ref[me, me]

    def choose(index, options):
        out = options[0][1]()
        for value, load in options[1:]:
            out = jnp.where(index == value, load(), out)
        return out

    for kv, src in enumerate((kx, vx)):
        for part, g in enumerate((ga, gb)):
            lo = part * half
            g[me, 0, kv] = src[lo : lo + half, :]
            g[me, 1, kv] = choose(
                start1,
                [
                    (j, lambda j=j: src[j * BLK + lo : j * BLK + lo + half, :])
                    for j in range(1, n_blocks)
                ],
            )
    owner = [gblk_ref[i] // n_blocks for i in range(GB)]
    place = [gblk_ref[i] % n_blocks for i in range(GB)]

    piece_rows = own_piece.shape[1]
    per = span // piece_rows
    pieces = [(i, kv, r) for i in range(GB) for kv in range(2) for r in range(per)]

    def send_candidates():
        for n, (i, kv, r) in enumerate(pieces):
            src = (kx, vx)[kv]
            lo = r * piece_rows
            own_piece[n] = choose(
                place[i],
                [
                    (j, lambda j=j: src[j * BLK + lo : j * BLK + lo + piece_rows, :])
                    for j in range(n_blocks)
                ],
            )
        got_z[z] = own_piece[z]
        for r in range(1, nz):
            zz = wrap(z + r, nz)
            c = remote(("g", r), own_piece.at[zz], got_z.at[z], {"ctx": zz * ny + y})
            c.start()
            sends.append(c)

    def pick_z():
        for r in range(1, nz):
            ref = got_z.at[wrap(z - r, nz)]
            remote(("g", r), ref, ref, {"ctx": ctx_at(-r, 0)}).wait_recv()
        o = owner[0]
        for i in range(1, GB):
            o = jnp.where(z >= i * (nz // GB), owner[i], o)
        got_y[y] = choose(o // ny, [(j, lambda j=j: got_z[j]) for j in range(nz)])

    def pick_y():
        r1.finish()
        o = owner[0]
        for i in range(1, GB):
            o = jnp.where(z >= i * (nz // GB), owner[i], o)
        picked_rows[z] = choose(o % ny, [(j, lambda j=j: got_y[j]) for j in range(ny)])

    def global_entries():
        r2.finish()

        def load(lo):
            out = []
            for kv in range(2):
                own = [n for n, q in enumerate(pieces) if q[1] == kv]
                out.append(jnp.concatenate([picked_rows[n] for n in own], axis=0)[lo : lo + half])
            return out

        return [
            (functools.partial(load, lo), [0.0] * PAGES_DEV) for lo in range(0, GROWS, half)
        ]

    waited = set()
    n_picked = [0]

    class Stream:
        def __init__(s, name, ref, axis, off, kind, far=0):
            s.name, s.ref, s.axis, s.off, s.kind, s.far = name, ref, axis, off, kind, far
            s.steps = (nz if axis == "z" else ny) // 2
            s.single = kind == "pages" and far != 0

        def place(s, rel):
            return (rel, s.off) if s.axis == "z" else (s.off, rel)

        def slot(s, rel):
            if s.kind == "rows":
                return s.ref.at[wrap(z + rel, nz) if s.axis == "z" else wrap(y + rel, ny)]
            return s.ref.at[ctx_at(*s.place(rel))]

        def to(s, d):
            return {"ctx": ctx_at(d, 0) if s.axis == "z" else ctx_at(0, d)}

        def hops(s, d):
            return s.steps if not s.far or d == s.far else s.steps - 1

        def picks(s, d, t):
            return s.single and t == s.hops(d) - 1

        def piece(s, rel, d, t):
            ref = s.slot(rel)
            if s.far:
                return ref.at[pl.ds(0, 1)] if s.picks(d, t) else ref
            if t == s.steps - 1:
                return ref.at[pl.ds(0 if d > 0 else 1, 1)]
            return ref

        def send(s, d, t):
            if t >= s.hops(d):
                return
            if t > 0:
                s.wait(d, t - 1)
            dst = s.piece(-d * t, d, t)
            src = dst
            if s.picks(d, t):
                k = n_picked[0]
                n_picked[0] += 1
                full = s.slot(-d * t)
                code = codes_ref[s.to(d)["ctx"], ctx_at(*s.place(-d * t))]
                for kv in range(2):
                    picked[k, 0, kv] = jnp.where(code % 2 == 0, full[1, kv], full[0, kv])
                src = picked.at[k]
            c = remote((s.name, d, t), src, dst, s.to(d))
            c.start()
            sends.append(c)

        def wait(s, d, t):
            if t >= s.hops(d) or (s.name, d, t) in waited:
                return
            waited.add((s.name, d, t))
            ref = s.piece(-d * (t + 1), d, t)
            remote((s.name, d, t), ref, ref, s.to(d)).wait_recv()

        def need(s, rel):
            if abs(rel) == s.steps:
                s.wait(1, s.steps - 1)
                s.wait(-1, s.steps - 1)
            elif rel < 0:
                s.wait(1, -rel - 1)
            elif rel > 0:
                s.wait(-1, rel - 1)

        def arrivals(s, t):
            out = []
            if t >= s.steps:
                return out
            if s.far or t < s.steps - 1:
                for d in (1, -1):
                    if t < s.hops(d):
                        out.append(page_entry(s, -d * (t + 1), s.picks(d, t)))
                        s.wait(d, t)
            else:
                s.wait(1, t)
                s.wait(-1, t)
                out.append(page_entry(s, s.steps, False))
            return out

        def finish(s):
            for d in (1, -1):
                for t in range(s.hops(d)):
                    s.wait(d, t)

    out_sems = [sem_id(("o", r)) for r in range(nh)]
    local = pltpu.make_async_copy(
        ob.at[row_slot(mh), :], out_ref.at[:, col_slot(mh)], recv_sem.at[out_sems[0]]
    )

    def hand_out(b):
        for h in range(n_heads):
            for lo in range(b * tile, (b + 1) * tile, BLK):
                at = slice(lo, lo + BLK)
                out = mixed[h, :, at] / totals[h, :, at]
                ob[at, h * HD : (h + 1) * HD] = out.T.astype(jnp.bfloat16)
        for p in range(b * tile // rl, (b + 1) * tile // rl):

            @pl.when(mh == p)
            def _():
                local.start()

            @pl.when(mh != p)
            def _():
                at = out_sems[0] + lax.rem(p - mh + nh, nh)
                pltpu.make_async_remote_copy(
                    src_ref=ob.at[row_slot(p), :],
                    dst_ref=out_ref.at[:, col_slot(mh)],
                    send_sem=send_sem.at[at],
                    recv_sem=recv_sem.at[at],
                    device_id={"head": jnp.int32(p)},
                    device_id_type=MESH,
                ).start()

    tile = 2 * BLK if rows % (2 * BLK) == 0 else rows

    def page_marks(n, first_row):
        row = lax.broadcasted_iota(jnp.int32, (n, HD), 0) + first_row
        page = jnp.where(row >= start1 * BLK, 1, 0)
        return page == lax.broadcasted_iota(jnp.int32, (n, HD), 1)

    def attend(n, keys, first=False, last=False):
        def block(b, carry):
            at = pl.ds(pl.multiple_of(b * tile, tile), tile)
            for h in range(n_heads):
                cols = slice(h * HD, (h + 1) * HD)
                s = lax.dot_general(
                    jnp.concatenate((keys[:n, cols], marks[:n, :]), axis=1),
                    jnp.concatenate((qx[at, cols], qmarks[at, :]), axis=1),
                    (((1,), (1,)), ((), ())),
                    preferred_element_type=jnp.float32,
                )
                s = s * rate
                top = jnp.max(s, axis=0, keepdims=True)
                if not first:
                    before = tops[h, :, at]
                    top = jnp.maximum(before, top)
                w = jnp.exp2(s - top)
                total = jnp.sum(w, axis=0, keepdims=True)
                mix = jnp.dot(
                    vt[cols, :n], w.astype(jnp.bfloat16), preferred_element_type=jnp.float32
                )
                if not first:
                    decay = jnp.exp2(before - top)
                    total = totals[h, :, at] * decay + total
                    mix = mixed[h, :, at] * decay + mix
                totals[h, :, at] = total
                mixed[h, :, at] = mix
                tops[h, :, at] = top
            return carry

        if not last:
            lax.fori_loop(0, rows // tile, block, 0)
            return
        for b in range(rows // tile):
            block(b, 0)
            hand_out(b)

    lane = lax.broadcasted_iota(jnp.int32, (half, HD), 1)

    def absorb(entries, last=False):
        if not entries:
            return
        zero = jnp.zeros((half, width), jnp.bfloat16)
        if len(entries) % 2:
            entries = entries + [(lambda: (zero, zero), [MASKED] * PAGES_DEV)]
        for j in range(0, len(entries), 2):
            pair = []
            for i, (load, level) in enumerate(entries[j : j + 2], j):
                k, v = load()
                ks[i * half : (i + 1) * half, :] = k
                marks[i * half : (i + 1) * half, :] = jnp.where(
                    lane == 0, level[0], jnp.where(lane == 1, level[1], 0.0)
                ).astype(jnp.bfloat16)
                pair.append(v)
            vt[:, j * half : (j + 2) * half] = jnp.concatenate(pair, axis=0).T
        attend(len(entries) * half, ks, last=last)

    def page_entry(s, rel, single):
        ref = s.slot(rel)
        code = codes_ref[me, ctx_at(*s.place(rel))]

        def load():
            if single:
                return ref[0, 0], ref[0, 1]
            return [jnp.where(code % 2 == 0, ref[1, kv], ref[0, kv]) for kv in range(2)]

        level = [
            jnp.where((code + 1) // 2 == page + 1, 0.0, MASKED) for page in range(PAGES_DEV)
        ]
        return load, level

    def attend_own():
        qmarks[...] = jnp.where(page_marks(rows, 0), 1.0, 0.0).astype(jnp.bfloat16)
        marks[:rows, :] = jnp.where(
            page_marks(rows, 0) | (lax.broadcasted_iota(jnp.int32, (rows, HD), 1) >= PAGES_DEV),
            0.0,
            MASKED,
        ).astype(jnp.bfloat16)
        for b in range(n_blocks):
            at = slice(b * BLK, (b + 1) * BLK)
            vt[:, at] = vx[at, :].T
        attend(rows, kx, first=True)

    a1 = Stream("a1", ga, "z", 0, "pages")
    b1 = Stream("b1", gb, "y", 0, "pages")
    za, yb = ring_offsets(nz), ring_offsets(ny)
    a2 = {o: Stream(("a2", o), ga, "y", o, "pages", 1 - 2 * (i % 2)) for i, o in enumerate([0] + za)}
    b2 = {o: Stream(("b2", o), gb, "z", o, "pages", 1 - 2 * (i % 2)) for i, o in enumerate([0] + yb)}
    r1 = Stream("r1", got_y, "y", 0, "rows", 1)
    r2 = Stream("r2", picked_rows, "z", 0, "rows", -1)

    def pairs(offs):
        out = []
        while len(offs) > 3:
            out.append(offs[:2])
            offs = offs[2:]
        return out + ([offs] if offs else [])

    za, yb = pairs(za), pairs(yb)
    groups = [[[a1, b1], [a2[0], b2[0]]]]
    for i in range(max(len(za), len(yb))):
        az, by = (za[i] if i < len(za) else []), (yb[i] if i < len(yb) else [])
        g = [[] for _ in range(max(len(az), len(by)))]
        for part, offs in ((a2, az), (b2, by)):
            for k, o in enumerate(offs):
                g[k].append(part[o])
        groups.append(g)
    rounds = []
    for gi, g in enumerate(groups):
        for t in range(max(s.steps for e in g for s in e)):
            events = [[(s, t) for s in e] for e in g]
            if gi > 0 and t == 0 and len(rounds) > 1:
                for k, e in enumerate(events):
                    if k < len(rounds[-1]):
                        rounds[-1][k] += e
                    else:
                        rounds[-1].append(e)
            else:
                rounds.append(events)
    last = len(rounds) - 1
    z_round, y_round = min(2, last), min(6, last)
    row_streams = []

    def push_rows(everything=False):
        for entry in row_streams:
            while entry[1] < entry[0].steps:
                for d in (1, -1):
                    entry[0].send(d, entry[1])
                entry[1] += 1
                if not everything:
                    break

    def start(event):
        for s, t in event:
            if t == 0 and s.off != 0:
                (a1 if s.axis == "y" else b1).need(s.off)
            for d in (1, -1):
                s.send(d, t)

    def arrivals(event):
        out = []
        for s, t in event:
            out += s.arrivals(t)
        return out

    globals_done = False
    for n, events in enumerate(rounds):
        before = rounds[n - 1] if n > 0 else []
        together = n <= min(1, last)
        if together:
            for event in events:
                start(event)
        if n == 0:
            send_candidates()
        if n == z_round:
            pick_z()
            row_streams.append([r1, 0])
        if n == y_round:
            push_rows(True)
            pick_y()
            row_streams.append([r2, 0])
        if n == min(1, last):
            wait_q()
            attend_own()
        for k in range(max(len(events), len(before))):
            if not together and k < len(events):
                start(events[k])
            if k == 0:
                push_rows()
            arrived = arrivals(before[k]) if k < len(before) else []
            if n == y_round + 5 and k == 0:
                push_rows(True)
                arrived += global_entries()
                globals_done = True
            absorb(arrived)
    arrived = []
    for event in rounds[-1]:
        arrived += arrivals(event)
    if not globals_done:
        push_rows(True)
        arrived += global_entries()
    absorb(arrived, True)
    for s in [a1, b1, r1] + list(a2.values()) + list(b2.values()):
        s.finish()

    local.wait()
    for r in range(1, nh):
        slot = out_ref.at[:, col_slot(lax.rem(mh + nh - r, nh))]
        remote(("o", r), slot, slot, {"head": peers[r - 1]}).wait_recv()
        mine = ob.at[row_slot(peers[r - 1]), :]
        remote(("o", r), mine, mine, {"head": peers[r - 1]}).wait_send()
    for c in sends:
        c.wait_send()


def shards(nz, ny, nh, queries, keys, values, page_blocks, page_links, global_blocks):
    rl, full = queries.shape
    rows, width = rl * nh, full // nh
    n_ctx = nz * ny
    n_heads = width // HD
    half = BLK // 2
    span = GROWS // GB
    bf, f32 = jnp.bfloat16, jnp.float32
    reader = jnp.arange(PAGES_DEV, dtype=jnp.int32)[None, :, None]
    links = page_links.reshape(n_ctx, PAGES_DEV, -1)
    value = 1 + links % PAGES_DEV + PAGES_DEV * reader
    source = jnp.arange(n_ctx, dtype=jnp.int32)
    codes = jnp.sum(
        jnp.where((links // PAGES_DEV)[..., None] == source, value[..., None], 0), axis=(1, 2)
    )
    codes = jnp.where(source[:, None] == source, page_blocks[:, :1], codes)
    n_sems = 4 * nh + 3 * (nz + ny) + nz * ny * 2
    piece_rows = span * GB * 2 // nz
    most = max(rows, 16 * half)
    smem = pl.BlockSpec(memory_space=pltpu.SMEM)
    hbm = pl.BlockSpec(memory_space=pl.ANY)
    return pl.pallas_call(
        functools.partial(body, nz, ny, nh),
        out_shape=jax.ShapeDtypeStruct((rl, full), bf),
        in_specs=[smem, smem, hbm, hbm, hbm],
        out_specs=hbm,
        scratch_shapes=[
            pltpu.VMEM((rows, width), bf),
            pltpu.VMEM((rows, width), bf),
            pltpu.VMEM((rows, width), bf),
            pltpu.VMEM((n_ctx, PAGES_DEV, 2, half, width), bf),
            pltpu.VMEM((n_ctx, PAGES_DEV, 2, half, width), bf),
            pltpu.VMEM((2 * (nz + ny), 1, 2, half, width), bf),
            pltpu.VMEM((nz, piece_rows, width), bf),
            pltpu.VMEM((nz, piece_rows, width), bf),
            pltpu.VMEM((ny, piece_rows, width), bf),
            pltpu.VMEM((nz, piece_rows, width), bf),
            pltpu.VMEM((most, width), bf),
            pltpu.VMEM((width, most), bf),
            pltpu.VMEM((most, HD), bf),
            pltpu.VMEM((rows, HD), bf),
            pltpu.VMEM((n_heads, 1, rows), f32),
            pltpu.VMEM((n_heads, 1, rows), f32),
            pltpu.VMEM((n_heads, HD, rows), f32),
            pltpu.VMEM((rows, width), bf),
            pltpu.SemaphoreType.DMA((n_sems,)),
            pltpu.SemaphoreType.DMA((n_sems,)),
        ],
        compiler_params=pltpu.CompilerParams(
            collective_id=0, has_side_effects=True, vmem_limit_bytes=60 * 1024 * 1024
        ),
        name="page_attention",
    )(codes, global_blocks, queries, keys, values)


def solution(mesh):
    nh = mesh.shape["head"]
    ny = RING_Y
    nz = mesh.shape["ctx"] // ny
    return jax.shard_map(
        functools.partial(shards, nz, ny, nh),
        mesh=mesh,
        in_specs=(
            P(("ctx", "head"), None),
            P(("ctx", "head"), None),
            P(("ctx", "head"), None),
            P(),
            P(),
            P(),
        ),
        out_specs=P(("ctx", "head"), None),
        check_vma=False,
    )
```

```python
import functools

import jax
import jax.numpy as jnp
from jax import lax
from jax.experimental import pallas as pl
from jax.experimental.pallas import tpu as pltpu
from jax.sharding import PartitionSpec as P

HD = 128
BLK = 128
PAGES_DEV = 2
GROWS = 64
GB = 2
RING_Y = 8
MESH = pl.DeviceIdType.MESH
MASKED = -1e30
LOG2E = 1.4426950408889634


def ring_offsets(n):
    out = []
    for d in range(1, (n + 1) // 2):
        out += [d, -d]
    if n % 2 == 0:
        out.append(n // 2)
    return out


def body(
    nz,
    ny,
    nh,
    codes_ref,
    gblk_ref,
    q_ref,
    k_ref,
    v_ref,
    out_ref,
    qx,
    kx,
    vx,
    ga,
    gb,
    picked,
    own_piece,
    got_z,
    got_y,
    picked_rows,
    ks,
    vt,
    marks,
    qmarks,
    tops,
    totals,
    mixed,
    ob,
    send_sem,
    recv_sem,
):
    rows, width = qx.shape
    rl = rows // nh
    half = BLK // 2
    span = GROWS // GB
    n_heads = width // HD
    n_blocks = rows // BLK
    me = lax.axis_index("ctx")
    mh = lax.axis_index("head")
    z, y = me // ny, me % ny
    rate = HD**-0.5 * LOG2E

    def wrap(v, n):
        return lax.rem(v + 2 * n, n)

    def ctx_at(dz, dy):
        return wrap(z + dz, nz) * ny + wrap(y + dy, ny)

    neighbours = [ctx_at(0, 1), ctx_at(0, -1)] + [ctx_at(r, 0) for r in range(1, nz)]
    peers = [lax.rem(mh + r, nh) for r in range(1, nh)]
    barrier = pltpu.get_barrier_semaphore()
    for n in neighbours:
        pl.semaphore_signal(barrier, inc=1, device_id={"ctx": n}, device_id_type=MESH)
    for p in peers:
        pl.semaphore_signal(barrier, inc=1, device_id={"head": p}, device_id_type=MESH)
    pl.semaphore_wait(barrier, len(neighbours) + len(peers))

    sems = {}
    sends = []

    def sem_id(key):
        return sems.setdefault(key, len(sems))

    def remote(key, src, dst, device):
        k = sem_id(key)
        return pltpu.make_async_remote_copy(
            src_ref=src,
            dst_ref=dst,
            send_sem=send_sem.at[k],
            recv_sem=recv_sem.at[k],
            device_id=device,
            device_id_type=MESH,
        )

    def row_slot(h):
        return pl.ds(pl.multiple_of(h * rl, 16), rl)

    def col_slot(h):
        return pl.ds(pl.multiple_of(h * width, HD), width)

    def spread(name, src, dst):
        local = pltpu.make_async_copy(
            src.at[:, col_slot(mh)], dst.at[row_slot(mh), :], recv_sem.at[sem_id((name, 0))]
        )
        local.start()
        for r, p in enumerate(peers, 1):
            c = remote((name, r), src.at[:, col_slot(p)], dst.at[row_slot(mh), :], {"head": p})
            c.start()
            sends.append(c)

        def wait():
            local.wait()
            for r in range(1, nh):
                slot = dst.at[row_slot(lax.rem(mh + nh - r, nh)), :]
                remote((name, r), slot, slot, {"head": peers[r - 1]}).wait_recv()

        return wait

    wait_k = spread("k", k_ref, kx)
    wait_v = spread("v", v_ref, vx)
    wait_q = spread("q", q_ref, qx)
    start1 = codes_ref[me, me]

    def choose(index, options):
        out = options[0][1]()
        for value, load in options[1:]:
            out = jnp.where(index == value, load(), out)
        return out

    for kv, (src, wait) in enumerate(((kx, wait_k), (vx, wait_v))):
        wait()
        for part, g in enumerate((ga, gb)):
            lo = part * half
            g[me, 0, kv] = src[lo : lo + half, :]
            g[me, 1, kv] = choose(
                start1,
                [
                    (j, lambda j=j: src[j * BLK + lo : j * BLK + lo + half, :])
                    for j in range(1, n_blocks)
                ],
            )
    owner = [gblk_ref[i] // n_blocks for i in range(GB)]
    place = [gblk_ref[i] % n_blocks for i in range(GB)]

    piece_rows = own_piece.shape[1]
    per = span // piece_rows
    pieces = [(i, kv, r) for i in range(GB) for kv in range(2) for r in range(per)]

    def send_candidates():
        for n, (i, kv, r) in enumerate(pieces):
            src = (kx, vx)[kv]
            lo = r * piece_rows
            own_piece[n] = choose(
                place[i],
                [
                    (j, lambda j=j: src[j * BLK + lo : j * BLK + lo + piece_rows, :])
                    for j in range(n_blocks)
                ],
            )
        got_z[z] = own_piece[z]
        for r in range(1, nz):
            zz = wrap(z + r, nz)
            c = remote(("g", r), own_piece.at[zz], got_z.at[z], {"ctx": zz * ny + y})
            c.start()
            sends.append(c)

    def pick_z():
        for r in range(1, nz):
            ref = got_z.at[wrap(z - r, nz)]
            remote(("g", r), ref, ref, {"ctx": ctx_at(-r, 0)}).wait_recv()
        o = owner[0]
        for i in range(1, GB):
            o = jnp.where(z >= i * (nz // GB), owner[i], o)
        got_y[y] = choose(o // ny, [(j, lambda j=j: got_z[j]) for j in range(nz)])

    def pick_y():
        r1.finish()
        o = owner[0]
        for i in range(1, GB):
            o = jnp.where(z >= i * (nz // GB), owner[i], o)
        picked_rows[z] = choose(o % ny, [(j, lambda j=j: got_y[j]) for j in range(ny)])

    def global_entries():
        r2.finish()

        def load(lo):
            out = []
            for kv in range(2):
                own = [n for n, q in enumerate(pieces) if q[1] == kv]
                out.append(jnp.concatenate([picked_rows[n] for n in own], axis=0)[lo : lo + half])
            return out

        return [
            (functools.partial(load, lo), [0.0] * PAGES_DEV) for lo in range(0, GROWS, half)
        ]

    waited = set()
    n_picked = [0]

    class Stream:
        def __init__(s, name, ref, axis, off, kind, far=0):
            s.name, s.ref, s.axis, s.off, s.kind, s.far = name, ref, axis, off, kind, far
            s.steps = (nz if axis == "z" else ny) // 2
            s.single = kind == "pages" and far != 0

        def place(s, rel):
            return (rel, s.off) if s.axis == "z" else (s.off, rel)

        def slot(s, rel):
            if s.kind == "rows":
                return s.ref.at[wrap(z + rel, nz) if s.axis == "z" else wrap(y + rel, ny)]
            return s.ref.at[ctx_at(*s.place(rel))]

        def to(s, d):
            return {"ctx": ctx_at(d, 0) if s.axis == "z" else ctx_at(0, d)}

        def hops(s, d):
            return s.steps if not s.far or d == s.far else s.steps - 1

        def picks(s, d, t):
            return s.single and t == s.hops(d) - 1

        def piece(s, rel, d, t):
            ref = s.slot(rel)
            if s.far:
                return ref.at[pl.ds(0, 1)] if s.picks(d, t) else ref
            if t == s.steps - 1:
                return ref.at[pl.ds(0 if d > 0 else 1, 1)]
            return ref

        def send(s, d, t):
            if t >= s.hops(d):
                return
            if t > 0:
                s.wait(d, t - 1)
            dst = s.piece(-d * t, d, t)
            src = dst
            if s.picks(d, t):
                k = n_picked[0]
                n_picked[0] += 1
                full = s.slot(-d * t)
                code = codes_ref[s.to(d)["ctx"], ctx_at(*s.place(-d * t))]
                for kv in range(2):
                    picked[k, 0, kv] = jnp.where(code % 2 == 0, full[1, kv], full[0, kv])
                src = picked.at[k]
            c = remote((s.name, d, t), src, dst, s.to(d))
            c.start()
            sends.append(c)

        def wait(s, d, t):
            if t >= s.hops(d) or (s.name, d, t) in waited:
                return
            waited.add((s.name, d, t))
            ref = s.piece(-d * (t + 1), d, t)
            remote((s.name, d, t), ref, ref, s.to(d)).wait_recv()

        def need(s, rel):
            if abs(rel) == s.steps:
                s.wait(1, s.steps - 1)
                s.wait(-1, s.steps - 1)
            elif rel < 0:
                s.wait(1, -rel - 1)
            elif rel > 0:
                s.wait(-1, rel - 1)

        def arrivals(s, t):
            out = []
            if t >= s.steps:
                return out
            if s.far or t < s.steps - 1:
                for d in (1, -1):
                    if t < s.hops(d):
                        out.append(page_entry(s, -d * (t + 1), s.picks(d, t)))
                        s.wait(d, t)
            else:
                s.wait(1, t)
                s.wait(-1, t)
                out.append(page_entry(s, s.steps, False))
            return out

        def finish(s):
            for d in (1, -1):
                for t in range(s.hops(d)):
                    s.wait(d, t)

    out_sems = [sem_id(("o", r)) for r in range(nh)]
    local = pltpu.make_async_copy(
        ob.at[row_slot(mh), :], out_ref.at[:, col_slot(mh)], recv_sem.at[out_sems[0]]
    )

    def hand_out(b):
        for h in range(n_heads):
            for lo in range(b * tile, (b + 1) * tile, BLK):
                at = slice(lo, lo + BLK)
                out = mixed[h, :, at] * (1.0 / totals[h, :, at])
                ob[at, h * HD : (h + 1) * HD] = out.T.astype(jnp.bfloat16)
        for p in range(b * tile // rl, (b + 1) * tile // rl):

            @pl.when(mh == p)
            def _():
                local.start()

            @pl.when(mh != p)
            def _():
                at = out_sems[0] + lax.rem(p - mh + nh, nh)
                pltpu.make_async_remote_copy(
                    src_ref=ob.at[row_slot(p), :],
                    dst_ref=out_ref.at[:, col_slot(mh)],
                    send_sem=send_sem.at[at],
                    recv_sem=recv_sem.at[at],
                    device_id={"head": jnp.int32(p)},
                    device_id_type=MESH,
                ).start()

    tile = 2 * BLK if rows % (2 * BLK) == 0 else rows

    def page_marks(n, first_row):
        row = lax.broadcasted_iota(jnp.int32, (n, HD), 0) + first_row
        page = jnp.where(row >= start1 * BLK, 1, 0)
        return page == lax.broadcasted_iota(jnp.int32, (n, HD), 1)

    def attend(n, keys, first=False, last=False):
        def block(b, carry):
            at = pl.ds(pl.multiple_of(b * tile, tile), tile)
            for h in range(n_heads):
                cols = slice(h * HD, (h + 1) * HD)
                s = lax.dot_general(
                    jnp.concatenate((keys[:n, cols], marks[:n, :]), axis=1),
                    jnp.concatenate((qx[at, cols], qmarks[at, :]), axis=1),
                    (((1,), (1,)), ((), ())),
                    preferred_element_type=jnp.float32,
                )
                s = s * rate
                top = jnp.max(s, axis=0, keepdims=True)
                if not first:
                    before = tops[h, :, at]
                    top = jnp.maximum(before, top)
                w = jnp.exp2(s - top)
                total = jnp.sum(w, axis=0, keepdims=True)
                mix = jnp.dot(
                    vt[cols, :n], w.astype(jnp.bfloat16), preferred_element_type=jnp.float32
                )
                if not first:
                    decay = jnp.exp2(before - top)
                    total = totals[h, :, at] * decay + total
                    mix = mixed[h, :, at] * decay + mix
                totals[h, :, at] = total
                mixed[h, :, at] = mix
                tops[h, :, at] = top
            return carry

        if not last:
            lax.fori_loop(0, rows // tile, block, 0)
            return
        for b in range(rows // tile):
            block(b, 0)
            hand_out(b)

    lane = lax.broadcasted_iota(jnp.int32, (half, HD), 1)

    def absorb(entries, last=False):
        if not entries:
            return
        zero = jnp.zeros((half, width), jnp.bfloat16)
        if len(entries) % 2:
            entries = entries + [(lambda: (zero, zero), [MASKED] * PAGES_DEV)]
        for j in range(0, len(entries), 2):
            pair = []
            for i, (load, level) in enumerate(entries[j : j + 2], j):
                k, v = load()
                ks[i * half : (i + 1) * half, :] = k
                marks[i * half : (i + 1) * half, :] = jnp.where(
                    lane == 0, level[0], jnp.where(lane == 1, level[1], 0.0)
                ).astype(jnp.bfloat16)
                pair.append(v)
            vt[:, j * half : (j + 2) * half] = jnp.concatenate(pair, axis=0).T
        attend(len(entries) * half, ks, last=last)

    def page_entry(s, rel, single):
        ref = s.slot(rel)
        code = codes_ref[me, ctx_at(*s.place(rel))]

        def load():
            if single:
                return ref[0, 0], ref[0, 1]
            return [jnp.where(code % 2 == 0, ref[1, kv], ref[0, kv]) for kv in range(2)]

        level = [
            jnp.where((code + 1) // 2 == page + 1, 0.0, MASKED) for page in range(PAGES_DEV)
        ]
        return load, level

    def attend_own():
        qmarks[...] = jnp.where(page_marks(rows, 0), 1.0, 0.0).astype(jnp.bfloat16)
        marks[:rows, :] = jnp.where(
            page_marks(rows, 0) | (lax.broadcasted_iota(jnp.int32, (rows, HD), 1) >= PAGES_DEV),
            0.0,
            MASKED,
        ).astype(jnp.bfloat16)
        for b in range(n_blocks):
            at = slice(b * BLK, (b + 1) * BLK)
            vt[:, at] = vx[at, :].T
        attend(rows, kx, first=True)

    a1 = Stream("a1", ga, "z", 0, "pages")
    b1 = Stream("b1", gb, "y", 0, "pages")
    za, yb = ring_offsets(nz), ring_offsets(ny)
    a2 = {o: Stream(("a2", o), ga, "y", o, "pages", 1 - 2 * (i % 2)) for i, o in enumerate([0] + za)}
    b2 = {o: Stream(("b2", o), gb, "z", o, "pages", 1 - 2 * (i % 2)) for i, o in enumerate([0] + yb)}
    r1 = Stream("r1", got_y, "y", 0, "rows", 1)
    r2 = Stream("r2", picked_rows, "z", 0, "rows", -1)

    def pairs(offs):
        out = []
        while len(offs) > 3:
            out.append(offs[:2])
            offs = offs[2:]
        return out + ([offs] if offs else [])

    za, yb = pairs(za), pairs(yb)
    groups = [[[a1, b1], [a2[0], b2[0]]]]
    for i in range(max(len(za), len(yb))):
        az, by = (za[i] if i < len(za) else []), (yb[i] if i < len(yb) else [])
        g = [[] for _ in range(max(len(az), len(by)))]
        for part, offs in ((a2, az), (b2, by)):
            for k, o in enumerate(offs):
                g[k].append(part[o])
        groups.append(g)
    rounds = []
    for gi, g in enumerate(groups):
        for t in range(max(s.steps for e in g for s in e)):
            events = [[(s, t) for s in e] for e in g]
            if gi > 0 and t == 0 and len(rounds) > 1:
                for k, e in enumerate(events):
                    if k < len(rounds[-1]):
                        rounds[-1][k] += e
                    else:
                        rounds[-1].append(e)
            else:
                rounds.append(events)
    last = len(rounds) - 1
    z_round, y_round = min(2, last), min(6, last)
    row_streams = []

    def push_rows(everything=False):
        for entry in row_streams:
            while entry[1] < entry[0].steps:
                for d in (1, -1):
                    entry[0].send(d, entry[1])
                entry[1] += 1
                if not everything:
                    break

    def start(event):
        for s, t in event:
            if t == 0 and s.off != 0:
                (a1 if s.axis == "y" else b1).need(s.off)
            for d in (1, -1):
                s.send(d, t)

    def arrivals(event):
        out = []
        for s, t in event:
            out += s.arrivals(t)
        return out

    globals_done = False
    for n, events in enumerate(rounds):
        before = rounds[n - 1] if n > 0 else []
        together = n <= min(1, last)
        if together:
            for event in events:
                start(event)
        if n == 0:
            send_candidates()
        if n == z_round:
            pick_z()
            row_streams.append([r1, 0])
        if n == y_round:
            push_rows(True)
            pick_y()
            row_streams.append([r2, 0])
        if n == min(1, last):
            wait_q()
            attend_own()
        for k in range(max(len(events), len(before))):
            if not together and k < len(events):
                start(events[k])
            if k == 0:
                push_rows()
            arrived = arrivals(before[k]) if k < len(before) else []
            if n == y_round + 5 and k == 0:
                push_rows(True)
                arrived += global_entries()
                globals_done = True
            absorb(arrived)
    arrived = []
    for event in rounds[-1]:
        arrived += arrivals(event)
    if not globals_done:
        push_rows(True)
        arrived += global_entries()
    absorb(arrived, True)
    for s in [a1, b1, r1] + list(a2.values()) + list(b2.values()):
        s.finish()

    local.wait()
    for r in range(1, nh):
        slot = out_ref.at[:, col_slot(lax.rem(mh + nh - r, nh))]
        remote(("o", r), slot, slot, {"head": peers[r - 1]}).wait_recv()
        mine = ob.at[row_slot(peers[r - 1]), :]
        remote(("o", r), mine, mine, {"head": peers[r - 1]}).wait_send()
    for c in sends:
        c.wait_send()


def shards(nz, ny, nh, queries, keys, values, page_blocks, page_links, global_blocks):
    rl, full = queries.shape
    rows, width = rl * nh, full // nh
    n_ctx = nz * ny
    n_heads = width // HD
    half = BLK // 2
    span = GROWS // GB
    bf, f32 = jnp.bfloat16, jnp.float32
    reader = jnp.arange(PAGES_DEV, dtype=jnp.int32)[None, :, None]
    links = page_links.reshape(n_ctx, PAGES_DEV, -1)
    value = 1 + links % PAGES_DEV + PAGES_DEV * reader
    source = jnp.arange(n_ctx, dtype=jnp.int32)
    codes = jnp.sum(
        jnp.where((links // PAGES_DEV)[..., None] == source, value[..., None], 0), axis=(1, 2)
    )
    codes = jnp.where(source[:, None] == source, page_blocks[:, :1], codes)
    n_sems = 4 * nh + 3 * (nz + ny) + nz * ny * 2
    piece_rows = span * GB * 2 // nz
    most = max(rows, 16 * half)
    smem = pl.BlockSpec(memory_space=pltpu.SMEM)
    hbm = pl.BlockSpec(memory_space=pl.ANY)
    return pl.pallas_call(
        functools.partial(body, nz, ny, nh),
        out_shape=jax.ShapeDtypeStruct((rl, full), bf),
        in_specs=[smem, smem, hbm, hbm, hbm],
        out_specs=hbm,
        scratch_shapes=[
            pltpu.VMEM((rows, width), bf),
            pltpu.VMEM((rows, width), bf),
            pltpu.VMEM((rows, width), bf),
            pltpu.VMEM((n_ctx, PAGES_DEV, 2, half, width), bf),
            pltpu.VMEM((n_ctx, PAGES_DEV, 2, half, width), bf),
            pltpu.VMEM((2 * (nz + ny), 1, 2, half, width), bf),
            pltpu.VMEM((nz, piece_rows, width), bf),
            pltpu.VMEM((nz, piece_rows, width), bf),
            pltpu.VMEM((ny, piece_rows, width), bf),
            pltpu.VMEM((nz, piece_rows, width), bf),
            pltpu.VMEM((most, width), bf),
            pltpu.VMEM((width, most), bf),
            pltpu.VMEM((most, HD), bf),
            pltpu.VMEM((rows, HD), bf),
            pltpu.VMEM((n_heads, 1, rows), f32),
            pltpu.VMEM((n_heads, 1, rows), f32),
            pltpu.VMEM((n_heads, HD, rows), f32),
            pltpu.VMEM((rows, width), bf),
            pltpu.SemaphoreType.DMA((n_sems,)),
            pltpu.SemaphoreType.DMA((n_sems,)),
        ],
        compiler_params=pltpu.CompilerParams(
            collective_id=0, has_side_effects=True, vmem_limit_bytes=60 * 1024 * 1024
        ),
        name="page_attention",
    )(codes, global_blocks, queries, keys, values)


def solution(mesh):
    nh = mesh.shape["head"]
    ny = RING_Y
    nz = mesh.shape["ctx"] // ny
    return jax.shard_map(
        functools.partial(shards, nz, ny, nh),
        mesh=mesh,
        in_specs=(
            P(("ctx", "head"), None),
            P(("ctx", "head"), None),
            P(("ctx", "head"), None),
            P(),
            P(),
            P(),
        ),
        out_specs=P(("ctx", "head"), None),
        check_vma=False,
    )
```
